256 devices in a mesh: outer: 16 (over z_hi, y, core), inner: 16 (over x, z_lo).
Axes of the slice: x: 4, y: 4, z: 8 (z_hi: 2, z_lo: 4; z = z_hi * 4 + z_lo), core: 2. Of those that a mesh axis runs over, the one named last changes fastest.
Arguments:
- queries: bfloat16 [32768, 4096], P(('outer', 'inner')), may hold values from -40 to 40
- keys: bfloat16 [32768, 512], P(('outer', 'inner')), may hold values from -4 to 4
- values: bfloat16 [32768, 512], P(('outer', 'inner')), may hold values from -6 to 6
- doc_lengths: int32 [16], replicated, may hold values from 1 to 8192, 32768 in all
Outputs:
- attended: bfloat16 [32768, 4096], P(('outer', 'inner'))
The draws below stay inside these ranges and needn't reach their ends.
All inputs are finite; a program needn't handle non-finite values.
Results may differ from the reference program's by a relative error of at most 0.005.
Values may be sent and summed in bfloat16 or wider, within the bound.
A program may use at most 256 MiB of HBM per device.

```python
import math
import jax
import jax.numpy as jnp
import numpy as np
from jax import lax

HEADS = 32
GROUPS = 4
HEAD_DIM = 128
TOK_DEV = 128
DOCS = 16
OUTER_STEPS = 2
SEQ = 32768
N_INNER = 16


def common_draw(key):
    base_key = jax.random.fold_in(key, 7)
    keys = jnp.clip(jax.random.normal(jax.random.fold_in(base_key, 1), (SEQ, GROUPS * HEAD_DIM), jnp.float32), -4.0, 4.0)
    queries = jnp.clip(jax.random.normal(jax.random.fold_in(base_key, 2), (SEQ, HEADS * HEAD_DIM), jnp.float32), -4.0, 4.0)
    return (queries, keys)


def draw_queries(key, part):
    return common_draw(key)[0].astype(jnp.bfloat16)


def draw_keys(key, part):
    return common_draw(key)[1].astype(jnp.bfloat16)


def steps_of(own_key, extent, cuts, low, largest):
    factor_of, own = 1.0, jax.random.fold_in(own_key, 6)
    for dim, shards_of in cuts:
        draws = jnp.exp(jax.random.uniform(jax.random.fold_in(own, dim), (shards_of,), jnp.float32, low / len(cuts), largest / len(cuts)))
        factor_of = factor_of * jnp.repeat(draws, extent[dim] // shards_of).reshape([-1 if axis == dim else 1 for axis in range(len(extent))])
    return factor_of


def length_profile(number_of, total, most, lean):
    loads = [(1 << 20) // math.isqrt(grade ** lean) + 1 for grade in range(2, number_of + 1)]
    surplus, counts = total - most - (number_of - 1), [1] * (number_of - 1)
    while surplus > 0:
        candidates = [i for i in range(number_of - 1) if counts[i] < most]
        pool, budget = sum([loads[i] for i in candidates]), surplus
        for i in candidates:
            more = min(most - counts[i], max(1, budget * loads[i] // pool), surplus)
            counts[i] = counts[i] + more
            surplus = surplus - more
    return np.array([most] + counts)


def ragged(key, amount, total, bound, lean):
    if amount == 2:
        one = jax.random.randint(key, (), max(1, total - bound), min(bound, total - 1) + 1)
        return jnp.stack([one, total - one])
    sizes = jnp.asarray(length_profile(amount, total, bound, lean), jnp.int32)
    couples = (amount - 1) // 2
    source_of, receiver = sizes[1:1 + 2 * couples:2], sizes[2:2 + 2 * couples:2]
    slack = jnp.minimum(source_of - 1, bound - receiver)
    moved = jax.random.randint(jax.random.fold_in(key, 1), (couples,), 0, 1 << 20) % (slack + 1)
    sizes = sizes.at[1:1 + 2 * couples:2].set(source_of - moved).at[2:2 + 2 * couples:2].set(receiver + moved)
    return sizes[jax.random.permutation(jax.random.fold_in(key, 2), amount)]


def bell_draw(stream_key, dims, deviation, most, pieces=(), kind=jnp.bfloat16):
    entries = deviation * jax.random.normal(stream_key, dims, jnp.float32)
    if pieces:
        entries = entries * steps_of(stream_key, dims, pieces, -0.22, 0.18)
    return jnp.clip(entries, -most, most).astype(kind)


def setup_inputs(seed: int = 0) -> dict:
    streams_of = jax.random.split(jax.random.key(seed), 5)
    queries = draw_queries(jax.random.fold_in(streams_of[4], 71), 0)
    keys = draw_keys(jax.random.fold_in(streams_of[4], 71), 0)
    values = bell_draw(streams_of[2], (SEQ, GROUPS * HEAD_DIM), 1.0, 6.0, ((0, 256),))
    doc_lengths = ragged(streams_of[3], DOCS, SEQ, SEQ // 4, 1).astype(jnp.int32)
    return dict(queries=queries, keys=keys, values=values, doc_lengths=doc_lengths)


def doc_of(positions, ends):
    return jnp.sum((positions[:, None] >= ends[None, :]).astype(jnp.int32), axis=1)


def reference(queries, keys, values, doc_lengths):
    seq = queries.shape[0]
    per_group = HEADS // GROUPS
    block = TOK_DEV * N_INNER
    span = (OUTER_STEPS + 1) * block
    margin = OUTER_STEPS * block
    scale = HEAD_DIM ** -0.5
    ends = jnp.cumsum(doc_lengths).astype(jnp.int32)
    key_pad = jnp.concatenate([jnp.zeros((margin, GROUPS * HEAD_DIM), keys.dtype), keys], 0)
    value_pad = jnp.concatenate([jnp.zeros((margin, GROUPS * HEAD_DIM), values.dtype), values], 0)
    query_blocks = queries.reshape(seq // TOK_DEV, TOK_DEV, GROUPS, per_group, HEAD_DIM)

    def one_block(index):
        query_rows = query_blocks[index].astype(jnp.float32)
        qpos = (index * TOK_DEV + jnp.arange(TOK_DEV, dtype=jnp.int32)).astype(jnp.int32)
        first = ((index // N_INNER) - OUTER_STEPS) * block
        first = first.astype(jnp.int32)
        key_rows = lax.dynamic_slice_in_dim(key_pad, (first + margin).astype(jnp.int32), span, 0).astype(jnp.float32).reshape(span, GROUPS, HEAD_DIM)
        value_rows = lax.dynamic_slice_in_dim(value_pad, (first + margin).astype(jnp.int32), span, 0).astype(jnp.float32).reshape(span, GROUPS, HEAD_DIM)
        kpos = (first + jnp.arange(span, dtype=jnp.int32)).astype(jnp.int32)
        allowed = (kpos[None, :] <= qpos[:, None]) & (kpos[None, :] >= 0) & (doc_of(kpos, ends)[None, :] == doc_of(qpos, ends)[:, None])
        scores = jnp.einsum("qghd,kgd->qghk", query_rows, key_rows) * scale
        scores = jnp.where(allowed[:, None, None, :], scores, jnp.float32(-1e30))
        top = jnp.max(scores, axis=3, keepdims=True)
        weights = jnp.where(allowed[:, None, None, :], jnp.exp(scores - top), jnp.float32(0.0))
        total = jnp.sum(weights, axis=3)
        rounded = weights.astype(jnp.bfloat16).astype(jnp.float32)
        mixed = jnp.einsum("qghk,kgd->qghd", rounded, value_rows)
        result = mixed / total[:, :, :, None]
        return result.astype(jnp.bfloat16).reshape(TOK_DEV, HEADS * HEAD_DIM)

    outputs = lax.map(one_block, jnp.arange(seq // TOK_DEV, dtype=jnp.int32))
    return outputs.reshape(seq, HEADS * HEAD_DIM)
```

```python
import functools
import math

import jax
import jax.numpy as jnp
from jax import lax
from jax.experimental import pallas as pl
from jax.experimental.pallas import tpu as pltpu
from jax.sharding import PartitionSpec as P

HEADS = 32
GROUPS = 4
PER = HEADS // GROUPS
D = 128
TOK = 128
BLOCK = 2048
DOCS = 16
BIG = 2.0**100
SCALE = math.log2(math.e) / math.sqrt(D)
MESH = pl.DeviceIdType.MESH
NT = (((1,), (1,)), ((), ()))
WIDE = 1024
NARROW = 512
ROWS = 256


def kernel(
    lens, q_hbm, k_hbm, v_hbm, out_hbm,
    qin, qa, kv, km, m_ref, acc, obuf,
    s_x, r_x, s_q, r_q, s_z, r_z, s_y, r_y, s_w, r_w, s_c, r_c, s_o, r_o,
):
    o = lax.axis_index("outer")
    i = lax.axis_index("inner")
    x, z = i // 4, i % 4
    c = o % 2

    def at(dx=0, dz=0, do=0):
        return (o + do, ((x + dx) % 4) * 4 + (z + dz) % 4)

    partner = (o + 1 - 2 * c, i)
    has_next = o < 14
    has_prev = o >= 2

    barrier = pltpu.get_barrier_semaphore()
    for d in (1, 2, 3):
        pl.semaphore_signal(barrier, 1, device_id=at(dx=d), device_id_type=MESH)
        pl.semaphore_signal(barrier, 1, device_id=at(dz=d), device_id_type=MESH)
    pl.semaphore_signal(barrier, 1, device_id=partner, device_id_type=MESH)
    pl.semaphore_signal(barrier, 1, device_id=((o + 2) % 16, i), device_id_type=MESH)
    pl.semaphore_signal(barrier, 1, device_id=((o + 14) % 16, i), device_id_type=MESH)
    pl.semaphore_wait(barrier, 9)

    def remote(src, dst, ss, rs, dev):
        return pltpu.make_async_remote_copy(
            src_ref=src, dst_ref=dst, send_sem=ss, recv_sem=rs, device_id=dev, device_id_type=MESH
        )

    def cols(ref, g, width):
        return ref.at[:, pl.ds(pl.multiple_of(g * width, width), width)]

    xs, qs = [], []
    for d in (1, 2, 3):
        g = (x + d) % 4
        xs.append(remote(cols(k_hbm, g, D), kv.at[0, x, z, :, 0:D], s_x.at[d, 0], r_x.at[d, 0], at(dx=d)))
        xs.append(remote(cols(v_hbm, g, D), kv.at[0, x, z, :, D:2 * D], s_x.at[d, 1], r_x.at[d, 1], at(dx=d)))
    for cp in xs:
        cp.start()
    for d in (1, 2, 3):
        g = (x + d) % 4
        qs.append(remote(cols(q_hbm, g, PER * D), qin.at[d], s_q.at[d], r_q.at[d], at(dx=d)))
    for cp in qs:
        cp.start()
    local = [
        pltpu.make_async_copy(cols(k_hbm, x, D), kv.at[0, x, z, :, 0:D], r_x.at[0, 0]),
        pltpu.make_async_copy(cols(v_hbm, x, D), kv.at[0, x, z, :, D:2 * D], r_x.at[0, 1]),
        pltpu.make_async_copy(cols(q_hbm, x, PER * D), qin.at[0], r_q.at[0]),
    ]
    for cp in local:
        cp.start()

    lane = lax.broadcasted_iota(jnp.int32, (1, D), 1)
    start_of = jnp.zeros((1, D), jnp.int32)
    end_of = jnp.zeros((1, D), jnp.int32)
    at_token = jnp.int32(0)
    for n in range(DOCS):
        start_of = jnp.where(lane == n, at_token, start_of)
        at_token = at_token + lens[n]
        end_of = jnp.where(lane == n, at_token, end_of)

    for slot in range(3):
        def mask_rows(t, carry, slot=slot):
            base = pl.multiple_of(t * 256, 256)
            pos = (o - slot) * BLOCK + base + lax.broadcasted_iota(jnp.int32, (256, D), 0)
            here = (pos >= start_of) & (pos < end_of)
            km[slot, pl.ds(base, 256), :] = jnp.where(here, 0.0, -BIG).astype(jnp.bfloat16)
            return carry

        lax.fori_loop(0, BLOCK // 256, mask_rows, 0)

    @pl.when(jnp.logical_not(has_prev))
    def _():
        kv[2] = jnp.zeros(kv.shape[1:], kv.dtype)

    @pl.when(o == 0)
    def _():
        kv[1] = jnp.zeros(kv.shape[1:], kv.dtype)

    for cp in local[:2]:
        cp.wait()
    for cp in xs:
        cp.wait_recv()
    zs = [remote(kv.at[0, :, z], kv.at[0, :, z], s_z.at[d], r_z.at[d], at(dz=d)) for d in (1, 2, 3)]
    for cp in zs:
        cp.start()
    ys = remote(kv.at[0, :, z], kv.at[2, :, z], s_y, r_y, (o + 2, i))

    @pl.when(has_next)
    def _():
        ys.start()

    ws = [remote(kv.at[2, :, z], kv.at[2, :, z], s_w.at[d], r_w.at[d], at(dz=d)) for d in (1, 2, 3)]

    @pl.when(has_prev)
    def _():
        ys.wait_recv()
        for cp in ws:
            cp.start()

    for cp in zs:
        cp.wait_recv()

    give_own = remote(kv.at[0], kv.at[1], s_c, r_c, partner)
    give_old = remote(kv.at[2], kv.at[1], s_c, r_c, partner)

    @pl.when(c == 0)
    def _():
        give_own.start()

    @pl.when(has_prev)
    def _():
        for cp in ws:
            cp.wait_recv()

    @pl.when((c == 1) & has_prev)
    def _():
        give_old.start()

    @pl.when((c == 1) | has_prev)
    def _():
        give_own.wait_recv()

    diag_rows = lax.broadcasted_iota(jnp.int32, (TOK, NARROW), 0)
    diag_cols = lax.broadcasted_iota(jnp.int32, (TOK, NARROW), 1)
    causal = jnp.where(diag_cols <= diag_rows + z * TOK, 0.0, -BIG)
    ones = jnp.where(lax.broadcasted_iota(jnp.int32, (WIDE, D), 1) == 0, 1.0, 0.0).astype(jnp.bfloat16)

    def tile(d, slot, first, size, diag):
        pieces = size // NARROW
        key_value = kv[slot, pl.ds(first // NARROW, pieces)].reshape(size, 2 * D)
        mask = km[slot, pl.ds(pl.multiple_of(first, NARROW), size), :]
        keys = jnp.concatenate([key_value[:, :D], mask], axis=1)
        values = jnp.concatenate([key_value[:, D:], ones[:size]], axis=1)
        for r in range(PER * TOK // ROWS):
            rows = pl.ds(r * ROWS, ROWS)
            s = lax.dot_general(qa[d, rows, :], keys, NT, preferred_element_type=jnp.float32)
            if diag:
                s = s + jnp.concatenate([causal] * (ROWS // TOK), axis=0)
            old = m_ref[rows, :]
            new = jnp.maximum(old, jnp.max(s, axis=1, keepdims=True) * SCALE)
            w = jnp.exp2(s * SCALE - jnp.tile(new, (1, size // D)))
            fade = jnp.exp2(old - new)
            m_ref[rows, :] = new
            mixed = jnp.dot(w.astype(jnp.bfloat16), values, preferred_element_type=jnp.float32)
            acc[rows, :] = acc[rows, :] * jnp.tile(fade, (1, 2)) + mixed

    outs = []
    for d in range(4):
        j = (x - d + 4) % 4
        if d == 0:
            local[2].wait()
        else:
            qs[d - 1].wait_recv()
        qpos = o * BLOCK + (j * 4 + z) * TOK + lax.broadcasted_iota(jnp.int32, (TOK, D), 0)
        mine = jnp.where((qpos >= start_of) & (qpos < end_of), 1.0, 0.0).astype(jnp.bfloat16)
        for h in range(PER):
            qa[d, h * TOK:(h + 1) * TOK, :D] = qin[d, :, h * D:(h + 1) * D]
            qa[d, h * TOK:(h + 1) * TOK, D:] = mine
        m_ref[...] = jnp.full(m_ref.shape, -BIG, jnp.float32)
        acc[...] = jnp.zeros(acc.shape, jnp.float32)
        tile(d, 0, j * NARROW, NARROW, True)

        def near(t, carry, d=d):
            tile(d, 0, t * NARROW, NARROW, False)
            return carry

        lax.fori_loop(0, j, near, 0)

        def far(t, carry, d=d):
            tile(d, 1 + t // (BLOCK // WIDE), (t % (BLOCK // WIDE)) * WIDE, WIDE, False)
            return carry

        lax.fori_loop(0, 2 * BLOCK // WIDE, far, 0)
        for h in range(PER):
            part = acc[h * TOK:(h + 1) * TOK, :]
            obuf[d, :, h * D:(h + 1) * D] = (part[:, :D] / part[:, D:D + 1]).astype(jnp.bfloat16)
        dst = cols(out_hbm, x, PER * D)
        if d == 0:
            cp = pltpu.make_async_copy(obuf.at[0], dst, r_o.at[0])
        else:
            cp = remote(obuf.at[d], dst, s_o.at[d], r_o.at[d], at(dx=4 - d))
        cp.start()
        outs.append(cp)

    for cp in outs:
        cp.wait()
    for cp in xs + qs:
        cp.wait_send()
    for cp in zs:
        cp.wait_send()

    @pl.when(has_next)
    def _():
        ys.wait_send()

    @pl.when(has_prev)
    def _():
        for cp in ws:
            cp.wait_send()

    @pl.when((c == 0) | has_prev)
    def _():
        give_own.wait_send()


def body(queries, keys, values, doc_lengths):
    any_ref = pl.BlockSpec(memory_space=pl.ANY)
    dma = pltpu.SemaphoreType.DMA
    bf16, f32 = jnp.bfloat16, jnp.float32
    return pl.pallas_call(
        kernel,
        out_shape=jax.ShapeDtypeStruct(queries.shape, bf16),
        in_specs=[pl.BlockSpec(memory_space=pltpu.SMEM), any_ref, any_ref, any_ref],
        out_specs=any_ref,
        scratch_shapes=[
            pltpu.VMEM((4, TOK, PER * D), bf16),
            pltpu.VMEM((4, PER * TOK, 2 * D), bf16),
            pltpu.VMEM((3, 4, 4, TOK, 2 * D), bf16),
            pltpu.VMEM((3, BLOCK, D), bf16),
            pltpu.VMEM((PER * TOK, D), f32),
            pltpu.VMEM((PER * TOK, 2 * D), f32),
            pltpu.VMEM((4, TOK, PER * D), bf16),
            dma((4, 2)), dma((4, 2)), dma((4,)), dma((4,)), dma((4,)), dma((4,)), dma, dma,
            dma((4,)), dma((4,)), dma, dma, dma((4,)), dma((4,)),
        ],
        compiler_params=pltpu.CompilerParams(
            collective_id=0, has_side_effects=True, vmem_limit_bytes=48 << 20
        ),
        cost_estimate=pl.CostEstimate(flops=13 * 10**9, bytes_accessed=4 << 20, transcendentals=22 * 10**6),
        name="attend",
    )(doc_lengths, queries, keys, values)


def solution(mesh):
    rows = P(("outer", "inner"), None)
    return jax.shard_map(
        body, mesh=mesh, in_specs=(rows, rows, rows, P()), out_specs=rows, check_vma=False
    )
```

```python
import functools
import math

import jax
import jax.numpy as jnp
from jax import lax
from jax.experimental import pallas as pl
from jax.experimental.pallas import tpu as pltpu
from jax.sharding import PartitionSpec as P

HEADS = 32
GROUPS = 4
PER = HEADS // GROUPS
D = 128
TOK = 128
BLOCK = 2048
DOCS = 16
BIG = 2.0**100
SCALE = math.log2(math.e) / math.sqrt(D)
MESH = pl.DeviceIdType.MESH
NT = (((1,), (1,)), ((), ()))
WIDE = 1024
NARROW = 512
ROWS = 256


def kernel(
    lens, q_hbm, k_hbm, v_hbm, out_hbm,
    qin, qa, kv, km, m_ref, acc, obuf,
    s_x, r_x, s_q, r_q, s_z, r_z, s_y, r_y, s_h, r_h, s_w, r_w, s_c, r_c, s_o, r_o,
):
    o = lax.axis_index("outer")
    i = lax.axis_index("inner")
    x, z = i // 4, i % 4
    c = o % 2

    def at(dx=0, dz=0, do=0):
        return (o + do, ((x + dx) % 4) * 4 + (z + dz) % 4)

    partner = (o + 1 - 2 * c, i)
    has_prev = o >= 2
    send_far = (o % 8 >= 6) & (o < 14)
    send_near = o % 8 < 6
    from_far = (o % 8 < 2) & has_prev
    from_near = o % 8 >= 2

    barrier = pltpu.get_barrier_semaphore()
    for d in (1, 2, 3):
        pl.semaphore_signal(barrier, 1, device_id=at(dx=d), device_id_type=MESH)
        pl.semaphore_signal(barrier, 1, device_id=at(dz=d), device_id_type=MESH)
    pl.semaphore_signal(barrier, 1, device_id=partner, device_id_type=MESH)
    pl.semaphore_signal(barrier, 1, device_id=((o + 2) % 16, i), device_id_type=MESH)
    pl.semaphore_signal(barrier, 1, device_id=((o + 14) % 16, i), device_id_type=MESH)
    pl.semaphore_wait(barrier, 9)

    def remote(src, dst, ss, rs, dev):
        return pltpu.make_async_remote_copy(
            src_ref=src, dst_ref=dst, send_sem=ss, recv_sem=rs, device_id=dev, device_id_type=MESH
        )

    def arrived(ref, sem):
        pltpu.make_async_copy(ref, ref, sem).wait()

    def cols(ref, g, width):
        return ref.at[:, pl.ds(pl.multiple_of(g * width, width), width)]

    xs, qs = [], []
    for d in (1, 2, 3):
        g = (x + d) % 4
        xs.append(remote(cols(k_hbm, g, D), kv.at[0, x, z, :, 0:D], s_x.at[d, 0], r_x.at[x], at(dx=d)))
        xs.append(remote(cols(v_hbm, g, D), kv.at[0, x, z, :, D:2 * D], s_x.at[d, 1], r_x.at[x], at(dx=d)))
    local = [
        pltpu.make_async_copy(cols(k_hbm, x, D), kv.at[0, x, z, :, 0:D], r_x.at[x]),
        pltpu.make_async_copy(cols(v_hbm, x, D), kv.at[0, x, z, :, D:2 * D], r_x.at[x]),
        pltpu.make_async_copy(cols(q_hbm, x, PER * D), qin.at[0], r_q.at[0]),
    ]
    for cp in xs + local:
        cp.start()
    for d in (1, 2, 3):
        g = (x + d) % 4
        qs.append(remote(cols(q_hbm, g, PER * D), qin.at[d], s_q.at[d], r_q.at[d], at(dx=d)))
    for cp in qs:
        cp.start()

    lane = lax.broadcasted_iota(jnp.int32, (1, D), 1)
    start_of = jnp.zeros((1, D), jnp.int32)
    end_of = jnp.zeros((1, D), jnp.int32)
    at_token = jnp.int32(0)
    for n in range(DOCS):
        start_of = jnp.where(lane == n, at_token, start_of)
        at_token = at_token + lens[n]
        end_of = jnp.where(lane == n, at_token, end_of)

    def mask_rows(t, carry):
        base = pl.multiple_of((t % 8) * 256, 256)
        pos = (o - t // 8) * BLOCK + base + lax.broadcasted_iota(jnp.int32, (256, D), 0)
        here = (pos >= start_of) & (pos < end_of)
        km[t // 8, pl.ds(base, 256), :] = jnp.where(here, 0.0, -BIG).astype(jnp.bfloat16)
        return carry

    lax.fori_loop(0, 3 * BLOCK // 256, mask_rows, 0)
    m_ref[...] = jnp.full(m_ref.shape, -BIG, jnp.float32)
    acc[...] = jnp.zeros(acc.shape, jnp.float32)

    @pl.when(jnp.logical_not(has_prev))
    def _():
        kv[2] = jnp.zeros(kv.shape[1:], kv.dtype)

    @pl.when(o == 0)
    def _():
        kv[1] = jnp.zeros(kv.shape[1:], kv.dtype)

    zs, hs = [], []
    for p in range(4):
        arrived(kv.at[0, p, z], r_x.at[p])
        for d in (1, 2, 3):
            cp = remote(kv.at[0, p, z], kv.at[0, p, z], s_z.at[d, p], r_z.at[d, p], at(dz=d))
            cp.start()
            zs.append(cp)
        hs.append(remote(kv.at[0, p, z], kv.at[2, p, z], s_h.at[p], r_h.at[p], (o + 2, i)))

    @pl.when(send_far)
    def _():
        for cp in hs:
            cp.start()

    def on_y(p):
        return remote(kv.at[0, p], kv.at[2, p], s_y.at[p], r_y.at[p], (o + 2, i))

    def on_w(p, d):
        return remote(kv.at[2, p, z], kv.at[2, p, z], s_w.at[d, p], r_w.at[d, p], at(dz=d))

    def give(p, slot):
        return remote(kv.at[slot, p], kv.at[1, p], s_c.at[p], r_c.at[p], partner)

    def wait_old(p):
        @pl.when(from_near)
        def _():
            arrived(kv.at[2, p], r_y.at[p])

        @pl.when(from_far)
        def _():
            for d in (1, 2, 3):
                arrived(kv.at[2, p, z], r_w.at[d, p])

    ones = jnp.where(lax.broadcasted_iota(jnp.int32, (WIDE, D), 1) == 0, 1.0, 0.0).astype(jnp.bfloat16)

    def tile(d, slot, first, size, bias=None):
        key_value = kv[slot, pl.ds(first // NARROW, size // NARROW)].reshape(size, 2 * D)
        mask = km[slot, pl.ds(pl.multiple_of(first, NARROW), size), :]
        keys = jnp.concatenate([key_value[:, :D], mask], axis=1)
        values = jnp.concatenate([key_value[:, D:], ones[:size]], axis=1)
        for r in range(PER * TOK // ROWS):
            rows = pl.ds(r * ROWS, ROWS)
            s = lax.dot_general(qa[d, rows, :], keys, NT, preferred_element_type=jnp.float32)
            if bias is not None:
                s = s + jnp.concatenate([bias] * (ROWS // TOK), axis=0)
            old = m_ref[d, rows, :]
            new = jnp.maximum(old, jnp.max(s, axis=1, keepdims=True) * SCALE)
            w = jnp.exp2(s * SCALE - jnp.tile(new, (1, size // D)))
            fade = jnp.exp2(old - new)
            m_ref[d, rows, :] = new
            mixed = jnp.dot(w.astype(jnp.bfloat16), values, preferred_element_type=jnp.float32)
            acc[d, rows, :] = acc[d, rows, :] * jnp.tile(fade, (1, 2)) + mixed

    ahead = lax.broadcasted_iota(jnp.int32, (TOK, NARROW), 1) - lax.broadcasted_iota(
        jnp.int32, (TOK, NARROW), 0
    )

    def own_piece(p, carry):
        for d in (1, 2, 3):
            arrived(kv.at[0, p, z], r_z.at[d, p])

        @pl.when(send_near)
        def _():
            on_y(p).start()

        @pl.when(c == 0)
        def _():
            give(p, 0).start()

        def own_chunk(d, carry):
            j = (x - d + 4) % 4

            @pl.when(p == 0)
            def _():
                arrived(qin.at[d], r_q.at[d])
                qpos = o * BLOCK + (j * 4 + z) * TOK + lax.broadcasted_iota(jnp.int32, (TOK, D), 0)
                mine = jnp.where((qpos >= start_of) & (qpos < end_of), 1.0, 0.0).astype(jnp.bfloat16)
                for h in range(PER):
                    qa[d, h * TOK:(h + 1) * TOK, :D] = qin[d, :, h * D:(h + 1) * D]
                    qa[d, h * TOK:(h + 1) * TOK, D:] = mine

            @pl.when(j >= p)
            def _():
                bias = jnp.where(ahead <= (j - p) * NARROW + z * TOK, 0.0, -BIG)
                tile(d, 0, p * NARROW, NARROW, bias)

            return carry

        lax.fori_loop(0, 4, own_chunk, 0)

        @pl.when(from_far)
        def _():
            arrived(kv.at[2, p, z], r_h.at[p])
            for d in (1, 2, 3):
                on_w(p, d).start()

        return carry

    lax.fori_loop(0, 4, own_piece, 0)

    def first_earlier(t, carry):
        for p in (2 * t, 2 * t + 1):
            @pl.when(c == 0)
            def _():
                wait_old(p)

            @pl.when(c == 1)
            def _():
                arrived(kv.at[1, p], r_c.at[p])

        def chunk(d, carry):
            tile(d, 2 - c, t * WIDE, WIDE)

            @pl.when((c == 1) & has_prev & (t == 0))
            def _():
                wait_old(d)
                give(d, 2).start()

            return carry

        return lax.fori_loop(0, 4, chunk, carry)

    lax.fori_loop(0, BLOCK // WIDE, first_earlier, 0)

    @pl.when((c == 0) & has_prev)
    def _():
        for p in range(4):
            arrived(kv.at[1, p], r_c.at[p])

    def send_out(d):
        return remote(obuf.at[d], cols(out_hbm, x, PER * D), s_o.at[d], r_o.at[d], at(dx=4 - d))

    keep = pltpu.make_async_copy(obuf.at[0], cols(out_hbm, x, PER * D), r_o.at[0])

    def last_earlier(n, carry):
        d = (n + 1) % 4

        def far(t, carry):
            tile(d, 1 + c, t * WIDE, WIDE)
            return carry

        lax.fori_loop(0, BLOCK // WIDE, far, 0)
        for h in range(PER):
            part = acc[d, h * TOK:(h + 1) * TOK, :]
            obuf[d, :, h * D:(h + 1) * D] = (part[:, :D] / part[:, D:D + 1]).astype(jnp.bfloat16)

        @pl.when(d > 0)
        def _():
            send_out(d).start()

        @pl.when(d == 0)
        def _():
            keep.start()

        return carry

    lax.fori_loop(0, 4, last_earlier, 0)

    keep.wait()
    for d in (1, 2, 3):
        send_out(d).wait()
    for cp in xs + qs + zs:
        cp.wait_send()

    @pl.when(send_near)
    def _():
        for p in range(4):
            on_y(p).wait_send()

    @pl.when(send_far)
    def _():
        for cp in hs:
            cp.wait_send()

    @pl.when(from_far)
    def _():
        for p in range(4):
            for d in (1, 2, 3):
                on_w(p, d).wait_send()

    @pl.when((c == 0) | has_prev)
    def _():
        for p in range(4):
            give(p, 0).wait_send()


def body(queries, keys, values, doc_lengths):
    any_ref = pl.BlockSpec(memory_space=pl.ANY)
    dma = pltpu.SemaphoreType.DMA
    bf16, f32 = jnp.bfloat16, jnp.float32
    return pl.pallas_call(
        kernel,
        out_shape=jax.ShapeDtypeStruct(queries.shape, bf16),
        in_specs=[pl.BlockSpec(memory_space=pltpu.SMEM), any_ref, any_ref, any_ref],
        out_specs=any_ref,
        scratch_shapes=[
            pltpu.VMEM((4, TOK, PER * D), bf16),
            pltpu.VMEM((4, PER * TOK, 2 * D), bf16),
            pltpu.VMEM((3, 4, 4, TOK, 2 * D), bf16),
            pltpu.VMEM((3, BLOCK, D), bf16),
            pltpu.VMEM((4, PER * TOK, D), f32),
            pltpu.VMEM((4, PER * TOK, 2 * D), f32),
            pltpu.VMEM((4, TOK, PER * D), bf16),
            dma((4, 2)), dma((4,)), dma((4,)), dma((4,)), dma((4, 4)), dma((4, 4)), dma((4,)), dma((4,)),
            dma((4,)), dma((4,)), dma((4, 4)), dma((4, 4)), dma((4,)), dma((4,)), dma((4,)), dma((4,)),
        ],
        compiler_params=pltpu.CompilerParams(
            collective_id=0, has_side_effects=True, vmem_limit_bytes=60 << 20
        ),
        cost_estimate=pl.CostEstimate(flops=13 * 10**9, bytes_accessed=4 << 20, transcendentals=22 * 10**6),
        name="attend",
    )(doc_lengths, queries, keys, values)


def solution(mesh):
    rows = P(("outer", "inner"), None)
    return jax.shard_map(
        body, mesh=mesh, in_specs=(rows, rows, rows, P()), out_specs=rows, check_vma=False
    )
```

```python
import functools
import math

import jax
import jax.numpy as jnp
from jax import lax
from jax.experimental import pallas as pl
from jax.experimental.pallas import tpu as pltpu
from jax.sharding import PartitionSpec as P

HEADS = 32
GROUPS = 4
PER = HEADS // GROUPS
D = 128
TOK = 128
BLOCK = 2048
DOCS = 16
BIG = 2.0**100
SCALE = math.log2(math.e) / math.sqrt(D)
MESH = pl.DeviceIdType.MESH
NT = (((1,), (1,)), ((), ()))
WIDE = 1024
NARROW = 512
ROWS = 512
CHUNK = PER * TOK


def kernel(
    lens, q_hbm, k_hbm, v_hbm, out_hbm,
    qin, qa, kv, km, m_ref, acc, obuf, held, ready,
    s_x, r_x, s_q, r_q, s_z, r_z, s_y, r_y, s_h, r_h, s_w, r_w, s_c, r_c, s_o, r_o,
):
    o = lax.axis_index("outer")
    i = lax.axis_index("inner")
    x, z = i // 4, i % 4
    c = o % 2

    def at(dx=0, dz=0):
        return (o, ((x + dx) % 4) * 4 + (z + dz) % 4)

    partner = (o + 1 - 2 * c, i)
    has_prev = o >= 2
    has_next = o < 14
    send_far = (o % 8 >= 6) & has_next
    send_near = o % 8 < 6
    from_far = (o % 8 < 2) & has_prev
    from_near = o % 8 >= 2
    relay = o >= 14
    mirror = x * 4 + 3 - z
    mz = 3 - z

    barrier = pltpu.get_barrier_semaphore()
    for d in (1, 2, 3):
        pl.semaphore_signal(barrier, 1, device_id=at(dx=d), device_id_type=MESH)
        pl.semaphore_signal(barrier, 1, device_id=at(dz=d), device_id_type=MESH)
    pl.semaphore_signal(barrier, 1, device_id=partner, device_id_type=MESH)

    @pl.when(has_next)
    def _():
        pl.semaphore_signal(
            barrier, 1, device_id=(o + 2, jnp.where(send_far, mirror, i)), device_id_type=MESH
        )

    @pl.when(send_far)
    def _():
        pl.semaphore_signal(barrier, 1, device_id=(o + 8, mirror), device_id_type=MESH)

    @pl.when(from_far)
    def _():
        for n in range(4):
            pl.semaphore_signal(barrier, 1, device_id=(o + 6, x * 4 + n), device_id_type=MESH)

    pl.semaphore_wait(barrier, 7 + jnp.where(has_prev, 1, 0) + jnp.where(relay, 5, 0))

    @pl.when(has_prev)
    def _():
        pl.semaphore_signal(
            ready, 1, device_id=(o - 2, jnp.where(from_far, mirror, i)), device_id_type=MESH
        )

    @pl.when(relay)
    def _():
        pl.semaphore_signal(ready, 1, device_id=(o - 8, mirror), device_id_type=MESH)

    def remote(src, dst, ss, rs, dev):
        return pltpu.make_async_remote_copy(
            src_ref=src, dst_ref=dst, send_sem=ss, recv_sem=rs, device_id=dev, device_id_type=MESH
        )

    def arrived(ref, sem):
        pltpu.make_async_copy(ref, ref, sem).wait()

    def cols(ref, g, width):
        return ref.at[:, pl.ds(pl.multiple_of(g * width, width), width)]

    xs, qs = [], []
    for d in (1, 2, 3):
        g = (x + d) % 4
        xs.append(remote(cols(k_hbm, g, D), kv.at[0, x, z, :, 0:D], s_x.at[d, 0], r_x.at[x], at(dx=d)))
        xs.append(remote(cols(v_hbm, g, D), kv.at[0, x, z, :, D:2 * D], s_x.at[d, 1], r_x.at[x], at(dx=d)))
    local = [
        pltpu.make_async_copy(cols(k_hbm, x, D), kv.at[0, x, z, :, 0:D], r_x.at[x]),
        pltpu.make_async_copy(cols(v_hbm, x, D), kv.at[0, x, z, :, D:2 * D], r_x.at[x]),
        pltpu.make_async_copy(cols(q_hbm, x, PER * D), qin.at[x], r_q.at[x]),
    ]
    for cp in xs + local:
        cp.start()
    for d in (1, 3, 2):
        g = (x + d) % 4
        qs.append(remote(cols(q_hbm, g, PER * D), qin.at[x], s_q.at[d], r_q.at[x], at(dx=d)))
    for cp in qs:
        cp.start()

    lane = lax.broadcasted_iota(jnp.int32, (1, D), 1)
    start_of = jnp.zeros((1, D), jnp.int32)
    end_of = jnp.zeros((1, D), jnp.int32)
    at_token = jnp.int32(0)
    for n in range(DOCS):
        start_of = jnp.where(lane == n, at_token, start_of)
        at_token = at_token + lens[n]
        end_of = jnp.where(lane == n, at_token, end_of)

    def mask_rows(t, carry):
        base = pl.multiple_of((t % 8) * 256, 256)
        pos = (o - t // 8) * BLOCK + base + lax.broadcasted_iota(jnp.int32, (256, D), 0)
        here = (pos >= start_of) & (pos < end_of)
        km[t // 8, pl.ds(base, 256), :] = jnp.where(here, 0.0, -BIG).astype(jnp.bfloat16)
        return carry

    lax.fori_loop(0, 3 * BLOCK // 256, mask_rows, 0)
    m_ref[...] = jnp.full(m_ref.shape, -BIG, jnp.float32)
    acc[...] = jnp.zeros(acc.shape, jnp.float32)

    @pl.when(jnp.logical_not(has_prev))
    def _():
        kv[2] = jnp.zeros(kv.shape[1:], kv.dtype)

    @pl.when(o == 0)
    def _():
        kv[1] = jnp.zeros(kv.shape[1:], kv.dtype)

    zs, hs = [], []
    for p in range(4):
        arrived(kv.at[0, p, z], r_x.at[p])
        if p == 0:
            @pl.when(has_next)
            def _():
                pl.semaphore_wait(ready, 1 + jnp.where(send_far, 1, 0))

        if p < 2:
            far = remote(kv.at[0, p, z], kv.at[2, p, z], s_h.at[p], r_h.at[p], (o + 2, mirror))
        else:
            far = remote(kv.at[0, p, z], held.at[p - 2], s_h.at[p], r_h.at[p], (o + 8, mirror))
        hs.append(far)

        @pl.when(send_far)
        def _():
            far.start()

        for d in (1, 2, 3):
            cp = remote(kv.at[0, p, z], kv.at[0, p, z], s_z.at[d, p], r_z.at[d, p], at(dz=d))
            cp.start()
            zs.append(cp)

    def on_y(p):
        return remote(kv.at[0, p], kv.at[2, p], s_y.at[p], r_y.at[p], (o + 2, i))

    def on_w(p, d):
        if p < 2:
            return remote(kv.at[2, p, mz], kv.at[2, p, mz], s_w.at[d, p], r_w.at[d, p], at(dz=d))
        to = (o - 6, x * 4 + (z + d) % 4)
        return remote(held.at[p - 2], kv.at[2, p, mz], s_w.at[d, p], r_w.at[d, p], to)

    def give(p, slot):
        return remote(kv.at[slot, p], kv.at[1, p], s_c.at[p], r_c.at[p], partner)

    def wait_old(p):
        @pl.when(from_near)
        def _():
            arrived(kv.at[2, p], r_y.at[p])

        @pl.when(from_far)
        def _():
            for d in (1, 2, 3) if p < 2 else (0, 1, 2, 3):
                arrived(kv.at[2, p, mz], r_w.at[d, p])

    ones = jnp.where(lax.broadcasted_iota(jnp.int32, (WIDE, D), 1) == 0, 1.0, 0.0).astype(jnp.bfloat16)

    def keys_of(slot, first, size):
        key_value = kv[slot, first // NARROW:(first + size) // NARROW].reshape(size, 2 * D)
        mask = km[slot, first:first + size, :]
        keys = jnp.concatenate([key_value[:, :D], mask], axis=1)
        values = jnp.concatenate([key_value[:, D:], ones[:size]], axis=1)
        return keys, values

    def steps(todo):
        def scores(n):
            rows, keys, values, bias = todo[n]
            s = lax.dot_general(qa[rows, :], keys, NT, preferred_element_type=jnp.float32)
            return s if bias is None else s + jnp.concatenate([bias] * (ROWS // TOK), axis=0)

        s = scores(0)
        for n in range(len(todo)):
            later = scores(n + 1) if n + 1 < len(todo) else None
            rows, keys, values, bias = todo[n]
            old = m_ref[rows, :]
            new = jnp.maximum(old, jnp.max(s, axis=1, keepdims=True) * SCALE)
            w = jnp.exp2(s * SCALE - jnp.tile(new, (1, s.shape[1] // D)))
            fade = jnp.exp2(old - new)
            m_ref[rows, :] = new
            mixed = jnp.dot(w.astype(jnp.bfloat16), values, preferred_element_type=jnp.float32)
            acc[rows, :] = acc[rows, :] * jnp.tile(fade, (1, 2)) + mixed
            s = later

    ahead = lax.broadcasted_iota(jnp.int32, (TOK, NARROW), 1) - lax.broadcasted_iota(
        jnp.int32, (TOK, NARROW), 0
    )
    causal = jnp.where(ahead <= z * TOK, 0.0, -BIG)

    def queries_in(d, carry):
        j = (x - d + 4) % 4
        arrived(qin.at[j], r_q.at[j])
        qpos = o * BLOCK + (j * 4 + z) * TOK + lax.broadcasted_iota(jnp.int32, (TOK, D), 0)
        mine = jnp.where((qpos >= start_of) & (qpos < end_of), 1.0, 0.0).astype(jnp.bfloat16)
        for h in range(PER):
            rows = pl.ds(pl.multiple_of(j * CHUNK + h * TOK, TOK), TOK)
            qa[rows, :D] = qin[j, :, h * D:(h + 1) * D]
            qa[rows, D:] = mine
        return carry

    def own(p):
        for d in (1, 2, 3):
            arrived(kv.at[0, p, z], r_z.at[d, p])

        @pl.when(send_near)
        def _():
            on_y(p).start()

        @pl.when(c == 0)
        def _():
            give(p, 0).start()

        if p == 0:
            lax.fori_loop(0, 4, queries_in, 0)
        if p == 3:
            @pl.when(from_far)
            def _():
                for n in (0, 1):
                    arrived(kv.at[2, n, mz], r_h.at[n])
                    for d in (1, 2, 3):
                        on_w(n, d).start()

            @pl.when(relay)
            def _():
                for n in (2, 3):
                    arrived(held.at[n - 2], r_h.at[n])
                    for d in (0, 1, 2, 3):
                        on_w(n, d).start()

        keys, values = keys_of(0, p * NARROW, NARROW)
        todo = []
        for r in range(p * CHUNK, 4 * CHUNK, ROWS):
            todo.append((slice(r, r + ROWS), keys, values, causal if r < (p + 1) * CHUNK else None))
        steps(todo)

    def earlier(p):
        @pl.when(c == 0)
        def _():
            wait_old(p)

        @pl.when(c == 1)
        def _():
            arrived(kv.at[1, p], r_c.at[p])

        @pl.when((c == 1) & has_prev)
        def _():
            for n in {0: (), 1: (0,), 2: (1,), 3: (2, 3)}[p]:
                wait_old(n)
                give(n, 2).start()

        keys, values = keys_of(2 - c, p * NARROW, NARROW)
        steps([(slice(r, r + ROWS), keys, values, None) for r in range(0, 4 * CHUNK, ROWS)])

    for p in range(4):
        own(p)
    for p in range(4):
        earlier(p)

    @pl.when((c == 0) & has_prev)
    def _():
        for p in range(4):
            arrived(kv.at[1, p], r_c.at[p])

    def send_out(d):
        return remote(obuf.at[d], cols(out_hbm, x, PER * D), s_o.at[d], r_o.at[d], at(dx=d))

    keep = pltpu.make_async_copy(obuf.at[0], cols(out_hbm, x, PER * D), r_o.at[0])

    def last(n, carry):
        d = jnp.where(n == 0, 2, jnp.where(n == 1, 1, jnp.where(n == 2, 3, 0)))
        base = ((x + d) % 4) * CHUNK
        todo = []
        for first in range(0, BLOCK, WIDE):
            keys, values = keys_of(1 + c, first, WIDE)
            for r in range(0, CHUNK, ROWS):
                todo.append((pl.ds(pl.multiple_of(base + r, ROWS), ROWS), keys, values, None))
        steps(todo)
        for h in range(PER):
            part = acc[pl.ds(pl.multiple_of(base + h * TOK, TOK), TOK), :]
            obuf[d, :, h * D:(h + 1) * D] = (part[:, :D] / part[:, D:D + 1]).astype(jnp.bfloat16)

        @pl.when(d > 0)
        def _():
            send_out(d).start()

        @pl.when(d == 0)
        def _():
            keep.start()

        return carry

    lax.fori_loop(0, 4, last, 0)

    keep.wait()
    for d in (1, 2, 3):
        send_out(d).wait()
    for cp in xs + qs + zs:
        cp.wait_send()

    @pl.when(send_near)
    def _():
        for p in range(4):
            on_y(p).wait_send()

    @pl.when(send_far)
    def _():
        for cp in hs:
            cp.wait_send()

    @pl.when(from_far)
    def _():
        for p in (0, 1):
            for d in (1, 2, 3):
                on_w(p, d).wait_send()

    @pl.when(relay)
    def _():
        for p in (2, 3):
            for d in (0, 1, 2, 3):
                on_w(p, d).wait_send()

    @pl.when((c == 0) | has_prev)
    def _():
        for p in range(4):
            give(p, 0).wait_send()


def body(queries, keys, values, doc_lengths):
    hbm = pl.BlockSpec(memory_space=pltpu.HBM)
    dma = pltpu.SemaphoreType.DMA
    bf16, f32 = jnp.bfloat16, jnp.float32
    return pl.pallas_call(
        kernel,
        out_shape=jax.ShapeDtypeStruct(queries.shape, bf16),
        in_specs=[pl.BlockSpec(memory_space=pltpu.SMEM), hbm, hbm, hbm],
        out_specs=pl.BlockSpec(memory_space=pltpu.VMEM),
        scratch_shapes=[
            pltpu.VMEM((4, TOK, PER * D), bf16),
            pltpu.VMEM((4 * CHUNK, 2 * D), bf16),
            pltpu.VMEM((3, 4, 4, TOK, 2 * D), bf16),
            pltpu.VMEM((3, BLOCK, D), bf16),
            pltpu.VMEM((4 * CHUNK, D), f32),
            pltpu.VMEM((4 * CHUNK, 2 * D), f32),
            pltpu.VMEM((4, TOK, PER * D), bf16),
            pltpu.VMEM((2, TOK, 2 * D), bf16),
            pltpu.SemaphoreType.REGULAR,
            dma((4, 2)), dma((4,)), dma((4,)), dma((4,)), dma((4, 4)), dma((4, 4)), dma((4,)), dma((4,)),
            dma((4,)), dma((4,)), dma((4, 4)), dma((4, 4)), dma((4,)), dma((4,)), dma((4,)), dma((4,)),
        ],
        compiler_params=pltpu.CompilerParams(
            collective_id=0, has_side_effects=True, vmem_limit_bytes=60 << 20
        ),
        cost_estimate=pl.CostEstimate(flops=13 * 10**9, bytes_accessed=4 << 20, transcendentals=22 * 10**6),
        name="attend",
    )(doc_lengths, queries, keys, values)


def solution(mesh):
    rows = P(("outer", "inner"), None)
    return jax.shard_map(
        body, mesh=mesh, in_specs=(rows, rows, rows, P()), out_specs=rows, check_vma=False
    )
```

```python
import functools
import math

import jax
import jax.numpy as jnp
from jax import lax
from jax.experimental import pallas as pl
from jax.experimental.pallas import tpu as pltpu
from jax.sharding import PartitionSpec as P

HEADS = 32
GROUPS = 4
PER = HEADS // GROUPS
D = 128
TOK = 128
BLOCK = 2048
DOCS = 16
BIG = 2.0**100
SCALE = math.log2(math.e) / math.sqrt(D)
MESH = pl.DeviceIdType.MESH
NT = (((1,), (1,)), ((), ()))
WIDE = 1024
NARROW = 512
ROWS = 512
CHUNK = PER * TOK


def kernel(
    lens, q_hbm, k_hbm, v_hbm, out_hbm,
    qin, qa, kv, km, m_ref, acc, obuf, held, ready,
    s_x, r_x, s_q, r_q, s_z, r_z, s_y, r_y, s_h, r_h, s_w, r_w, s_c, r_c, s_o, r_o,
):
    o = lax.axis_index("outer")
    i = lax.axis_index("inner")
    x, z = i // 4, i % 4
    c = o % 2

    def at(dx=0, dz=0):
        return (o, ((x + dx) % 4) * 4 + (z + dz) % 4)

    partner = (o + 1 - 2 * c, i)
    has_prev = o >= 2
    has_next = o < 14
    send_far = (o % 8 >= 6) & has_next
    send_near = o % 8 < 6
    from_far = (o % 8 < 2) & has_prev
    from_near = o % 8 >= 2
    relay = o >= 14
    mirror = x * 4 + 3 - z
    mz = 3 - z

    barrier = pltpu.get_barrier_semaphore()
    for d in (1, 2, 3):
        pl.semaphore_signal(barrier, 1, device_id=at(dx=d), device_id_type=MESH)
        pl.semaphore_signal(barrier, 1, device_id=at(dz=d), device_id_type=MESH)
    pl.semaphore_signal(barrier, 1, device_id=partner, device_id_type=MESH)

    @pl.when(has_next)
    def _():
        pl.semaphore_signal(
            barrier, 1, device_id=(o + 2, jnp.where(send_far, mirror, i)), device_id_type=MESH
        )

    @pl.when(send_far)
    def _():
        pl.semaphore_signal(barrier, 1, device_id=(o + 8, mirror), device_id_type=MESH)

    @pl.when(from_far)
    def _():
        for n in range(4):
            pl.semaphore_signal(barrier, 1, device_id=(o + 6, x * 4 + n), device_id_type=MESH)

    pl.semaphore_wait(barrier, 7 + jnp.where(has_prev, 1, 0) + jnp.where(relay, 5, 0))

    @pl.when(has_prev)
    def _():
        pl.semaphore_signal(
            ready, 1, device_id=(o - 2, jnp.where(from_far, mirror, i)), device_id_type=MESH
        )

    @pl.when(relay)
    def _():
        pl.semaphore_signal(ready, 1, device_id=(o - 8, mirror), device_id_type=MESH)

    def remote(src, dst, ss, rs, dev):
        return pltpu.make_async_remote_copy(
            src_ref=src, dst_ref=dst, send_sem=ss, recv_sem=rs, device_id=dev, device_id_type=MESH
        )

    def arrived(ref, sem):
        pltpu.make_async_copy(ref, ref, sem).wait()

    def cols(ref, g, width):
        return ref.at[:, pl.ds(pl.multiple_of(g * width, width), width)]

    xs, qs = [], []
    for d in (1, 2, 3):
        g = (x + d) % 4
        xs.append(remote(cols(k_hbm, g, D), kv.at[0, x, z, :, 0:D], s_x.at[d, 0], r_x.at[x], at(dx=d)))
        xs.append(remote(cols(v_hbm, g, D), kv.at[0, x, z, :, D:2 * D], s_x.at[d, 1], r_x.at[x], at(dx=d)))
    local = [
        pltpu.make_async_copy(cols(k_hbm, x, D), kv.at[0, x, z, :, 0:D], r_x.at[x]),
        pltpu.make_async_copy(cols(v_hbm, x, D), kv.at[0, x, z, :, D:2 * D], r_x.at[x]),
        pltpu.make_async_copy(cols(q_hbm, x, PER * D), qin.at[x], r_q.at[x]),
    ]
    for cp in xs + local:
        cp.start()
    for d in (1, 3, 2):
        g = (x + d) % 4
        qs.append(remote(cols(q_hbm, g, PER * D), qin.at[x], s_q.at[d], r_q.at[x], at(dx=d)))
    for cp in qs:
        cp.start()

    lane = lax.broadcasted_iota(jnp.int32, (1, D), 1)
    start_of = jnp.zeros((1, D), jnp.int32)
    end_of = jnp.zeros((1, D), jnp.int32)
    at_token = jnp.int32(0)
    for n in range(DOCS):
        start_of = jnp.where(lane == n, at_token, start_of)
        at_token = at_token + lens[n]
        end_of = jnp.where(lane == n, at_token, end_of)

    def mask_rows(t, carry):
        base = pl.multiple_of((t % 8) * 256, 256)
        pos = (o - t // 8) * BLOCK + base + lax.broadcasted_iota(jnp.int32, (256, D), 0)
        here = (pos >= start_of) & (pos < end_of)
        km[t // 8, pl.ds(base, 256), :] = jnp.where(here, 0.0, -BIG).astype(jnp.bfloat16)
        return carry

    lax.fori_loop(0, 3 * BLOCK // 256, mask_rows, 0)
    m_ref[...] = jnp.full(m_ref.shape, -BIG, jnp.float32)
    acc[...] = jnp.zeros(acc.shape, jnp.float32)

    @pl.when(jnp.logical_not(has_prev))
    def _():
        kv[2] = jnp.zeros(kv.shape[1:], kv.dtype)

    @pl.when(o == 0)
    def _():
        kv[1] = jnp.zeros(kv.shape[1:], kv.dtype)

    def on_y(p, d):
        part = (p, (z + d) % 4)
        return remote(kv.at[(0, *part)], kv.at[(2, *part)], s_y.at[d, p], r_y.at[p], (o + 2, i))

    zs, hs = [], []
    for p in range(4):
        arrived(kv.at[0, p, z], r_x.at[p])
        if p == 0:
            @pl.when(has_next)
            def _():
                pl.semaphore_wait(ready, 1 + jnp.where(send_far, 1, 0))

        if p < 2:
            far = remote(kv.at[0, p, z], kv.at[2, p, z], s_h.at[p], r_h.at[p], (o + 2, mirror))
        else:
            far = remote(kv.at[0, p, z], held.at[p - 2], s_h.at[p], r_h.at[p], (o + 8, mirror))
        hs.append(far)

        @pl.when(send_far)
        def _():
            far.start()

        @pl.when(send_near)
        def _():
            on_y(p, 0).start()

        for d in (1, 2, 3):
            zs.append(remote(kv.at[0, p, z], kv.at[0, p, z], s_z.at[d, p], r_z.at[d, p], at(dz=d)))

        @pl.when(jnp.logical_not(from_far) | (p < 2))
        def _():
            for cp in zs[3 * p:]:
                cp.start()

    def on_w(p, d):
        if p < 2:
            return remote(kv.at[2, p, mz], kv.at[2, p, mz], s_w.at[d, p], r_w.at[d, p], at(dz=d))
        to = (o - 6, x * 4 + (z + d) % 4)
        return remote(held.at[p - 2], kv.at[2, p, mz], s_w.at[d, p], r_w.at[d, p], to)

    def give(p, slot):
        return remote(kv.at[slot, p], kv.at[1, p], s_c.at[p], r_c.at[p], partner)

    def wait_old(p):
        @pl.when(from_near)
        def _():
            arrived(kv.at[2, p], r_y.at[p])

        @pl.when(from_far)
        def _():
            for d in (1, 2, 3):
                arrived(kv.at[2, p, mz], r_w.at[d, p])

        @pl.when(from_far & (p >= 2))
        def _():
            arrived(kv.at[2, p, mz], r_w.at[0, p])

    ones = jnp.where(lax.broadcasted_iota(jnp.int32, (WIDE, D), 1) == 0, 1.0, 0.0).astype(jnp.bfloat16)

    def keys_of(slot, piece, count=1):
        size = count * NARROW
        key_value = kv[slot, pl.ds(piece, count)].reshape(size, 2 * D)
        mask = km[slot, pl.ds(pl.multiple_of(piece * NARROW, NARROW), size), :]
        keys = jnp.concatenate([key_value[:, :D], mask], axis=1)
        values = jnp.concatenate([key_value[:, D:], ones[:size]], axis=1)
        return keys, values

    def steps(todo):
        def scores(n):
            rows, keys, values, bias = todo[n]
            s = lax.dot_general(qa[rows, :], keys, NT, preferred_element_type=jnp.float32)
            return s if bias is None else s + jnp.concatenate([bias] * (ROWS // TOK), axis=0)

        s = scores(0)
        for n in range(len(todo)):
            later = scores(n + 1) if n + 1 < len(todo) else None
            rows, keys, values, bias = todo[n]
            old = m_ref[rows, :]
            new = jnp.maximum(old, jnp.max(s, axis=1, keepdims=True) * SCALE)
            w = jnp.exp2(s * SCALE - jnp.tile(new, (1, s.shape[1] // D)))
            fade = jnp.exp2(old - new)
            m_ref[rows, :] = new
            mixed = jnp.dot(w.astype(jnp.bfloat16), values, preferred_element_type=jnp.float32)
            acc[rows, :] = acc[rows, :] * jnp.tile(fade, (1, 2)) + mixed
            s = later

    ahead = lax.broadcasted_iota(jnp.int32, (TOK, NARROW), 1) - lax.broadcasted_iota(
        jnp.int32, (TOK, NARROW), 0
    )
    causal = jnp.where(ahead <= z * TOK, 0.0, -BIG)

    def queries_in(d):
        j = (x - d + 4) % 4
        arrived(qin.at[j], r_q.at[j])
        qpos = o * BLOCK + (j * 4 + z) * TOK + lax.broadcasted_iota(jnp.int32, (TOK, D), 0)
        mine = jnp.where((qpos >= start_of) & (qpos < end_of), 1.0, 0.0).astype(jnp.bfloat16)
        for h in range(PER):
            rows = pl.ds(pl.multiple_of(j * CHUNK + h * TOK, TOK), TOK)
            qa[rows, :D] = qin[j, :, h * D:(h + 1) * D]
            qa[rows, D:] = mine

    def first_own(steps_back):
        for d in steps_back:
            queries_in(d)
        keys, values = keys_of(0, 0)
        todo = []
        for d in steps_back:
            j = (x - d + 4) % 4
            bias = jnp.where(ahead <= j * NARROW + z * TOK, 0.0, -BIG)
            for r in range(0, CHUNK, ROWS):
                todo.append((pl.ds(pl.multiple_of(j * CHUNK + r, ROWS), ROWS), keys, values, bias))
        steps(todo)

    def hand_on(p):
        @pl.when(from_far)
        def _():
            arrived(kv.at[2, p, mz], r_h.at[p])
            for d in (1, 2, 3):
                on_w(p, d).start()

        @pl.when(relay)
        def _():
            arrived(held.at[p], r_h.at[p + 2])
            for d in (0, 1, 2, 3):
                on_w(p + 2, d).start()

    def own(p):
        for d in (1, 2, 3):
            arrived(kv.at[0, p, z], r_z.at[d, p])

        @pl.when(send_near)
        def _():
            for d in (1, 2, 3):
                on_y(p, d).start()

        @pl.when(c == 0)
        def _():
            give(p, 0).start()

        if p == 0:
            hand_on(0)
            first_own((0, 1, 3))
            hand_on(1)

            @pl.when(from_far)
            def _():
                for cp in zs[6:]:
                    cp.start()

            first_own((2,))
            return
        keys, values = keys_of(0, p)
        todo = []
        for r in range(p * CHUNK, 4 * CHUNK, ROWS):
            todo.append((slice(r, r + ROWS), keys, values, causal if r < (p + 1) * CHUNK else None))
        steps(todo)

    def wait_first(p):
        @pl.when(c == 0)
        def _():
            wait_old(p)

        @pl.when(c == 1)
        def _():
            arrived(kv.at[1, p], r_c.at[p])

    def wait_second(p):
        @pl.when((c == 0) & has_prev)
        def _():
            arrived(kv.at[1, p], r_c.at[p])

    def earlier(n, carry):
        second = (n == 2) | (n == 4)
        p = jnp.where(n == 3, 2, jnp.where((n == 1) | (n == 4), 1, 0))

        @pl.when((c == 1) & has_prev & (n >= 1))
        def _():
            wait_old(n - 1)
            give(n - 1, 2).start()

        @pl.when(second)
        def _():
            wait_second(p)

        @pl.when(jnp.logical_not(second))
        def _():
            wait_first(p)

        slot = jnp.where(second, 1 + c, 2 - c)
        keys, values = keys_of(slot, p)
        steps([(slice(r, r + ROWS), keys, values, None) for r in range(0, 4 * CHUNK, ROWS)])
        return carry

    own(0)
    own(1)
    lax.fori_loop(0, jnp.where(from_far, 2, 1), earlier, 0)
    own(2)
    lax.fori_loop(jnp.where(from_far, 2, 1), 2, earlier, 0)
    own(3)
    lax.fori_loop(2, 5, earlier, 0)
    wait_first(3)
    wait_second(2)
    wait_second(3)

    half = PER * D // 2

    def span(n, width):
        return pl.ds(pl.multiple_of(n * width, width), width)

    def send_out(d, h):
        return remote(
            obuf.at[d, :, span(h, half)], out_hbm.at[:, span(2 * x + h, half)],
            s_o.at[d, h], r_o.at[d, h], at(dx=d),
        )

    def keep(h):
        return pltpu.make_async_copy(
            obuf.at[0, :, span(h, half)], out_hbm.at[:, span(2 * x + h, half)], r_o.at[0, h]
        )

    def last(n, carry):
        pairs = (
            (jnp.where(n == 0, 2, jnp.where(n == 3, 0, 1)), jnp.where(n == 2, 1, 0)),
            (jnp.where(n == 0, 2, jnp.where(n == 3, 0, 3)), jnp.where(n == 1, 0, 1)),
        )
        todo = []
        for keys, values in (keys_of(1 + c, 2, 2), keys_of(2 - c, 3)):
            for d, h in pairs:
                todo.append((span(((x + d) % 4) * 2 + h, ROWS), keys, values, None))
        steps(todo)
        for d, h in pairs:
            base = ((x + d) % 4) * CHUNK + h * ROWS
            for m in range(ROWS // TOK):
                part = acc[pl.ds(pl.multiple_of(base + m * TOK, TOK), TOK), :]
                to = pl.ds(pl.multiple_of(h * half + m * D, D), D)
                obuf[d, :, to] = (part[:, :D] / part[:, D:D + 1]).astype(jnp.bfloat16)

            @pl.when(d > 0)
            def _():
                send_out(d, h).start()

            @pl.when(d == 0)
            def _():
                keep(h).start()

        return carry

    lax.fori_loop(0, 4, last, 0)

    for h in (0, 1):
        keep(h).wait()
        for d in (1, 2, 3):
            send_out(d, h).wait()
    for cp in xs + qs + zs:
        cp.wait_send()

    @pl.when(send_near)
    def _():
        for p in range(4):
            for d in range(4):
                on_y(p, d).wait_send()

    @pl.when(send_far)
    def _():
        for cp in hs:
            cp.wait_send()

    @pl.when(from_far)
    def _():
        for p in (0, 1):
            for d in (1, 2, 3):
                on_w(p, d).wait_send()

    @pl.when(relay)
    def _():
        for p in (2, 3):
            for d in (0, 1, 2, 3):
                on_w(p, d).wait_send()

    @pl.when((c == 0) | has_prev)
    def _():
        for p in range(4):
            give(p, 0).wait_send()


def body(queries, keys, values, doc_lengths):
    hbm = pl.BlockSpec(memory_space=pltpu.HBM)
    dma = pltpu.SemaphoreType.DMA
    bf16, f32 = jnp.bfloat16, jnp.float32
    return pl.pallas_call(
        kernel,
        out_shape=jax.ShapeDtypeStruct(queries.shape, bf16),
        in_specs=[pl.BlockSpec(memory_space=pltpu.SMEM), hbm, hbm, hbm],
        out_specs=pl.BlockSpec(memory_space=pltpu.VMEM),
        scratch_shapes=[
            pltpu.VMEM((4, TOK, PER * D), bf16),
            pltpu.VMEM((4 * CHUNK, 2 * D), bf16),
            pltpu.VMEM((3, 4, 4, TOK, 2 * D), bf16),
            pltpu.VMEM((3, BLOCK, D), bf16),
            pltpu.VMEM((4 * CHUNK, D), f32),
            pltpu.VMEM((4 * CHUNK, 2 * D), f32),
            pltpu.VMEM((4, TOK, PER * D), bf16),
            pltpu.VMEM((2, TOK, 2 * D), bf16),
            pltpu.SemaphoreType.REGULAR,
            dma((4, 2)), dma((4,)), dma((4,)), dma((4,)), dma((4, 4)), dma((4, 4)), dma((4, 4)), dma((4,)),
            dma((4,)), dma((4,)), dma((4, 4)), dma((4, 4)), dma((4,)), dma((4,)), dma((4, 2)), dma((4, 2)),
        ],
        compiler_params=pltpu.CompilerParams(
            collective_id=0, has_side_effects=True, vmem_limit_bytes=48 << 20
        ),
        cost_estimate=pl.CostEstimate(flops=13 * 10**9, bytes_accessed=4 << 20, transcendentals=22 * 10**6),
        name="attend",
    )(doc_lengths, *(pltpu.with_memory_space_constraint(a, pltpu.HBM) for a in (queries, keys, values)))


def solution(mesh):
    rows = P(("outer", "inner"), None)
    return jax.shard_map(
        body, mesh=mesh, in_specs=(rows, rows, rows, P()), out_specs=rows, check_vma=False
    )
```
